256 devices in a mesh: tgt: 8 (over y, x_lo), src: 32 (over z, x_hi, core).
Axes of the slice: x: 4 (x_hi: 2, x_lo: 2; x = x_hi * 2 + x_lo), y: 4, z: 8, core: 2. Of those that a mesh axis runs over, the one named last changes fastest.
Arguments:
- history: bfloat16 [16384, 2048], P(('src', 'tgt')), may hold values from -6 to 6
- kernel: bfloat16 [16, 32, 512, 4096], P('tgt', 'src'), may hold values from -0.03125 to 0.03125
- delays: int32 [16, 32], P('tgt', 'src'), may hold values from 0 to 120
- tile_mask: int32 [16, 32], P('tgt', 'src'), may hold values 0 or 1
Outputs:
- incoming: float32 [16, 512, 1024], P('tgt', 'src')
The draws below stay inside these ranges and needn't reach their ends.
All inputs are finite; a program needn't handle non-finite values. No bound on the sum of `tile_mask` on one device may be relied on, other than what follows from the above.
Results may differ from the reference program's by a relative error of at most 0.0003.
Values may be sent and summed in bfloat16 or wider, within the bound.
No kernel may reach another device: no remote copies, remote signals or barrier semaphores. Data moves between devices by JAX's collectives and lax.ppermute only.
A program may use at most 64 MiB of HBM per device.

```python
import jax
import jax.numpy as jnp
from jax import lax

B = 512
TAPS = 8
H = 128
E = 16
S = 64
NT = 16
NS = 32


def plant(result, key, smallest, largest):
    shape = result.shape
    place = [jax.random.randint(jax.random.fold_in(key, axis), (), 0, shape[axis]) for axis in range(len(shape))]
    result = result.at[tuple(place)].set(smallest)
    longest = shape.index(max(shape))
    place[longest] = (place[longest] + 1) % shape[longest]
    return result.at[tuple(place)].set(largest)


def strengthened(result, own_key, source, target, parts, factor):
    def block_of(axis_at):
        return (jnp.arange(result.shape[axis_at]) // (result.shape[axis_at] // parts)).reshape((-1,) + (1,) * (result.ndim - 1 - axis_at))

    one_side = jax.random.permutation(own_key, parts)[block_of(target)]
    other_side = (block_of(target) + parts // 2) % parts
    return jnp.where((block_of(source) == one_side) | (block_of(source) == other_side), factor * result, result)


def block_levels(key, shape, split, low, largest):
    def one(axis_at, blocks):
        heights = jax.random.uniform(jax.random.fold_in(jax.random.fold_in(key, 6), axis_at), (blocks,), jnp.float32, low / len(split), largest / len(split))
        return jnp.repeat(jnp.exp(heights), shape[axis_at] // blocks).reshape((-1,) + (1,) * (len(shape) - axis_at - 1))

    factor_of = one(*split[0])
    for cut in split[1:]:
        factor_of = factor_of * one(*cut)
    return factor_of


def bell_draw(rng, shape, spread, bound, cuts=(), kind=jnp.bfloat16):
    entries = spread * jax.random.normal(rng, shape, jnp.float32)
    if cuts:
        entries = entries * block_levels(rng, shape, cuts, -0.22, 0.18)
    return jnp.clip(entries, -bound, bound).astype(kind)


def gaussian_with(rng, extent, width, most, cuts, heavy, kind=jnp.bfloat16):
    result = width * jax.random.normal(rng, extent, jnp.float32)
    if cuts:
        result = result * block_levels(rng, extent, cuts, -0.22, 0.18)
    return jnp.clip(strengthened(result, jax.random.fold_in(rng, 3), *heavy), -most, most).astype(kind)


def setup_inputs(seed: int = 0) -> dict:
    streams_of = jax.random.split(jax.random.key(seed), 5)
    history = bell_draw(streams_of[0], (NS * B, H * E), 1.0, 6.0, ((0, 256),))
    kernel = gaussian_with(streams_of[1], (NT, NS, B, TAPS * B), (TAPS * B * NS) ** -0.5, 0.03125, ((0, 8), (1, 32)), (1, 2, 32, 2.75))
    delays = plant(jax.random.randint(streams_of[2], (NT, NS), 0, 121), jax.random.fold_in(streams_of[2], 1), 0, 120).astype(jnp.int32)
    tile_mask = plant((jax.random.randint(streams_of[3], (NT, NS), 0, 4) < 3).astype(jnp.int32), jax.random.fold_in(streams_of[3], 1), 0, 1)
    return dict(history=history, kernel=kernel, delays=delays, tile_mask=tile_mask)


def tile_term(kernel_tile, source, tile_delay):
    padded = jnp.pad(source.reshape(B, H, E).astype(jnp.float32), ((0, 0), (0, S), (0, 0)))

    def window(tap_index):
        first_step = (H - tile_delay - tap_index).astype(jnp.int32)
        return lax.dynamic_slice(padded, (jnp.int32(0), first_step, jnp.int32(0)), (B, S, E))

    stacked = jax.vmap(window)(jnp.arange(TAPS, dtype=jnp.int32)).reshape(TAPS * B, S * E)
    return jnp.dot(kernel_tile.astype(jnp.float32), stacked, precision=lax.Precision.HIGHEST)


def reference(history, kernel, delays, tile_mask):
    blocks = history.reshape(NS, B, H * E)

    def target_row(inputs):
        kernel_row, delay_row, mask_row = inputs

        def add_tile(running, item):
            kernel_tile, source, tile_delay, tile_live = item
            return running + tile_live.astype(jnp.float32) * tile_term(kernel_tile, source, tile_delay), None

        running, _ = lax.scan(add_tile, jnp.zeros((B, S * E), jnp.float32), (kernel_row, blocks, delay_row, mask_row))
        return running

    return lax.map(target_row, (kernel, delays, tile_mask))
```

```python
import jax
import jax.numpy as jnp
import numpy as np
from jax import lax
from jax.experimental import pallas as pl
from jax.experimental.pallas import tpu as pltpu
from jax.sharding import Mesh, PartitionSpec as P

B = 512
TAPS = 8
H = 128
E = 16
S = 64
LANES = 128
COLS = S * E
WIDE = H * E
STEPS_PER_VREG = LANES // E

NY, NX, NZ, NH, NC = 4, 2, 8, 2, 2
AXES = ("y", "xl", "z", "xh", "c")
SHAPE = (NY, NX, NZ, NH, NC)
OFFSETS = (1, -1, 2, -2, 3, -3, 4)
GROUP = 16
BLOCK_ROWS = NH * 2 * GROUP
MESSAGE = BLOCK_ROWS * COLS // LANES


def route(move):
    index = np.arange(np.prod(SHAPE)).reshape(SHAPE)
    pairs = []
    for here in np.ndindex(*SHAPE):
        there = tuple(p % n for p, n in zip(move(*here), SHAPE))
        pairs.append((int(index[here]), int(index[there])))
    return pairs


def shift(x, dy=0, dx=0, dz=0, dh=0, dc=0):
    def move(y, xl, z, xh, c):
        return (y + dy, xl + dx, z + (dz if c == 0 else -dz), xh + dh, c + dc)

    return lax.ppermute(x, AXES, route(move))


def multiply_body(first, last, *refs):
    info, delays, live = refs[:3]
    low, high = refs[3:5]
    taps = refs[5 : 5 + TAPS]
    rest = refs[5 + TAPS :]
    if first:
        before, rest = None, rest
    else:
        before, rest = rest[0], rest[1:]
    if last:
        keep, send, shifted = rest
    else:
        after, shifted = rest
    tile = pl.program_id(0)

    @pl.when(tile == 0)
    def _():
        shifted[:, :, WIDE:] = jnp.zeros((STEPS_PER_VREG, LANES, COLS), jnp.bfloat16)
        for ref, place in ((low, info[1]), (high, 64 - info[1])):
            value = ref[...]
            at = pl.multiple_of(place, 64)
            for j in range(STEPS_PER_VREG):
                moved = value if j == 0 else jnp.concatenate([value[:, j * E :], jnp.zeros((64, j * E), jnp.bfloat16)], 1)
                shifted[j, pl.ds(at, 64), :WIDE] = moved

    delay = delays[tile]
    windows = []
    for tap in range(TAPS):
        step = H - delay - tap
        column = pl.multiple_of((step // STEPS_PER_VREG) * LANES, LANES)
        windows.append(shifted[step % STEPS_PER_VREG, :, pl.ds(column, COLS)])
    left = jnp.concatenate([tap[0, 0] for tap in taps], 1)
    total = jnp.dot(left, jnp.concatenate(windows, 0), preferred_element_type=jnp.float32)
    if before is not None:
        total = total + before[0]
    if not last:
        after[0] = total
        return
    total = total * live[tile].astype(jnp.float32)
    core = info[2]
    for z in range(NZ):
        for h in range(NH):
            row = ((z * NH + h) * NC) * GROUP
            one, two = total[row : row + GROUP], total[row + GROUP : row + 2 * GROUP]
            keep[z, h, 0] = jnp.where(core == 0, one, two)
            send[z, h, 0] = jnp.where(core == 0, two, one)


def multiply(info, delays, live, kernel, low, high, before, last):
    first = before is None

    def tap_spec(tap):
        return pl.BlockSpec((1, 1, B, LANES), lambda i, info, d, m: (i, 0, 0, tap * (B // LANES) + info[0]))

    half = pl.BlockSpec((64, WIDE), lambda i, *_: (0, 0))
    whole = pl.BlockSpec((1, B, COLS), lambda i, *_: (i, 0, 0))
    in_specs = [half, half] + [tap_spec(tap) for tap in range(TAPS)]
    operands = [low, high] + [kernel] * TAPS
    if not first:
        in_specs.append(whole)
        operands.append(before)
    if last:
        parts = pl.BlockSpec((NZ, NH, 1, GROUP, COLS), lambda i, *_: (0, 0, i, 0, 0))
        out_specs = [parts, parts]
        out_shape = [jax.ShapeDtypeStruct((NZ, NH, 2, GROUP, COLS), jnp.float32)] * 2
    else:
        out_specs = whole
        out_shape = jax.ShapeDtypeStruct((2, B, COLS), jnp.float32)
    return pl.pallas_call(
        lambda *refs: multiply_body(first, last, *refs),
        grid_spec=pltpu.PrefetchScalarGridSpec(
            num_scalar_prefetch=3,
            grid=(2,),
            in_specs=in_specs,
            out_specs=out_specs,
            scratch_shapes=[pltpu.VMEM((STEPS_PER_VREG, LANES, WIDE + COLS), jnp.bfloat16)],
        ),
        out_shape=out_shape,
        compiler_params=pltpu.CompilerParams(vmem_limit_bytes=40 << 20),
        name="multiply",
    )(info, delays, live, *operands)


def power_of_two(exponent):
    size = jnp.abs(exponent)
    result = jnp.ones(exponent.shape, jnp.float32)
    for bit in range(7):
        up, down = float(2.0 ** (1 << bit)), float(2.0 ** -(1 << bit))
        factor = jnp.where(exponent < 0, down, up)
        result = jnp.where((size >> bit) & 1 == 1, result * factor, result)
    return result


def encode_body(info, keep, get, own, *messages):
    z, sign = info[3], info[4]
    own[...] = keep[z] + get[z]
    for offset, message in zip(OFFSETS, messages):
        there = (z + sign * offset + NZ) % NZ
        scales = []
        for group in range(NH * 2):
            h, t = divmod(group, 2)
            value = keep[there, h, t] + get[there, h, t]
            peak = jnp.max(jnp.abs(value), axis=(0, 1), keepdims=True)
            peak = jnp.broadcast_to(peak, (1, LANES))
            exponent = jnp.ceil(jnp.log2(jnp.maximum(peak, 1e-30))).astype(jnp.int32) - 15
            scales.append(exponent)
            inverse = jnp.broadcast_to(power_of_two(-exponent), (GROUP, LANES))
            for j in range(COLS // LANES):
                scaled = jnp.clip(jnp.round(value[:, j * LANES : (j + 1) * LANES] * inverse), -32767.0, 32767.0)
                row = (group * (COLS // LANES) + j) * GROUP
                message[row : row + GROUP] = scaled.astype(jnp.int32).astype(jnp.int16)
        rows = lax.broadcasted_iota(jnp.int32, (GROUP, LANES), 0) // 4
        packed = jnp.zeros((GROUP, LANES), jnp.int32)
        for group, exponent in enumerate(scales):
            packed = jnp.where(rows == group, jnp.broadcast_to(exponent, (GROUP, LANES)), packed)
        message[MESSAGE:] = packed.astype(jnp.int16)


def encode(info, keep, get):
    return pl.pallas_call(
        encode_body,
        in_specs=[pl.BlockSpec(memory_space=pltpu.SMEM)] + [pl.BlockSpec(memory_space=pltpu.VMEM)] * 2,
        out_shape=[jax.ShapeDtypeStruct((NH, 2, GROUP, COLS), jnp.float32)]
        + [jax.ShapeDtypeStruct((MESSAGE + GROUP, LANES), jnp.int16)] * len(OFFSETS),
        compiler_params=pltpu.CompilerParams(vmem_limit_bytes=24 << 20),
        name="encode",
    )(info, keep, get)


def decode_body(info, own, *refs):
    messages, mine, other = refs[: len(OFFSETS)], refs[-2], refs[-1]
    units = []
    for message in messages:
        packed = message[MESSAGE:].astype(jnp.int32)
        units.append([power_of_two(packed[4 * group : 4 * group + 1]) for group in range(NH * 2)])
    for t in range(2):
        for j in range(COLS // LANES):
            sums = []
            for h in range(NH):
                group = h * 2 + t
                row = (group * (COLS // LANES) + j) * GROUP
                total = own[h, t, :, j * LANES : (j + 1) * LANES]
                for message, unit in zip(messages, units):
                    part = message[row : row + GROUP].astype(jnp.int32).astype(jnp.float32)
                    total = total + part * jnp.broadcast_to(unit[group], (GROUP, LANES))
                sums.append(total)
            here = info[5] == 0
            mine[t, :, j * LANES : (j + 1) * LANES] = jnp.where(here, sums[0], sums[1])
            other[t, :, j * LANES : (j + 1) * LANES] = jnp.where(here, sums[1], sums[0])


def decode(info, own, messages):
    return pl.pallas_call(
        decode_body,
        in_specs=[pl.BlockSpec(memory_space=pltpu.SMEM)] + [pl.BlockSpec(memory_space=pltpu.VMEM)] * (1 + len(OFFSETS)),
        out_shape=[jax.ShapeDtypeStruct((2, GROUP, COLS), jnp.float32)] * 2,
        compiler_params=pltpu.CompilerParams(vmem_limit_bytes=24 << 20),
        name="decode",
    )(info, own, *messages)


def body(history, kernel, delays, tile_mask):
    y, xl, z, xh, c = (lax.axis_index(name) for name in AXES)
    delays, live = delays[:, 0], tile_mask[:, 0]
    here = history
    two_far = shift(here, dy=2, dx=1)
    two = shift(here, dy=2)
    up_far = shift(here, dy=1, dx=1)
    up = shift(here, dy=1)
    down_far = shift(here, dy=-1, dx=1)
    down = shift(here, dy=-1)
    beside = shift(here, dx=1)

    def info(block):
        return jnp.stack([block % NY, xl * 64, c, z, 1 - 2 * c, xh]).astype(jnp.int32)

    total = None
    for block, low, high, last in (
        (y + 2, two, two_far, False),
        (y + 3, up, up_far, False),
        (y + 1, down, down_far, False),
        (y, here, beside, True),
    ):
        total = multiply(info(block), delays, live, kernel, low, high, total, last)
    keep, send = total
    get = shift(send, dc=1)
    own, *messages = encode(info(y), keep, get)
    received = [shift(message, dz=offset) for offset, message in zip(OFFSETS, messages)]
    mine, other = decode(info(y), own, received)
    return mine + shift(other, dh=1)


def solution(mesh):
    fine = Mesh(mesh.devices.reshape(SHAPE), AXES)
    tgt, src = ("y", "xl"), ("z", "xh", "c")
    placed = (
        P(src + tgt, None),
        P(tgt, src, None, None),
        P(tgt, src),
        P(tgt, src),
    )
    return jax.shard_map(body, mesh=fine, in_specs=placed, out_specs=P(tgt, src, None), check_vma=False)
```

```python
import jax
import jax.numpy as jnp
import numpy as np
from jax import lax
from jax.experimental import pallas as pl
from jax.experimental.pallas import tpu as pltpu
from jax.sharding import Mesh, PartitionSpec as P

B = 512
TAPS = 8
H = 128
E = 16
S = 64
LANES = 128
COLS = S * E
WIDE = H * E
STEPS_PER_VREG = LANES // E

NY, NX, NZ, NH, NC = 4, 2, 8, 2, 2
AXES = ("y", "xl", "z", "xh", "c")
SHAPE = (NY, NX, NZ, NH, NC)
OFFSETS = (1, -1, 2, -2, 3, -3, 4)
GROUP = 16
BLOCK_ROWS = NH * 2 * GROUP
MESSAGE = BLOCK_ROWS * COLS // LANES


def route(move):
    index = np.arange(np.prod(SHAPE)).reshape(SHAPE)
    pairs = []
    for here in np.ndindex(*SHAPE):
        there = tuple(p % n for p, n in zip(move(*here), SHAPE))
        pairs.append((int(index[here]), int(index[there])))
    return pairs


def shift(x, dy=0, dx=0, dz=0, dh=0, dc=0):
    def move(y, xl, z, xh, c):
        return (y + dy, xl + dx, z + (dz if c == 0 else -dz), xh + dh, c + dc)

    return lax.ppermute(x, AXES, route(move))


def multiply_body(turn, first, last, info, low, high, kernel, *rest):
    if first:
        after, staged, shifted, arrived = rest
        copies = [pltpu.make_async_copy(kernel.at[tile, 0], staged.at[tile], arrived.at[tile]) for tile in range(2)]
        for copy in copies:
            copy.start()
    elif last:
        before, keep, send, shifted = rest
        staged = kernel
    else:
        before, after, shifted = rest
        staged = kernel
    block = lax.rem(info[0] + turn, NY)
    shifted[:, :, WIDE:] = jnp.zeros((STEPS_PER_VREG, LANES, COLS), jnp.bfloat16)
    for ref, place in ((low, info[1]), (high, 64 - info[1])):
        value = ref[...]
        at = pl.multiple_of(place, 64)
        for j in range(STEPS_PER_VREG):
            moved = value if j == 0 else jnp.concatenate([value[:, j * E :], jnp.zeros((64, j * E), jnp.bfloat16)], 1)
            shifted[j, pl.ds(at, 64), :WIDE] = moved
    for tile in range(2):
        if first:
            copies[tile].wait()
        weights, windows = [], []
        for tap in range(TAPS):
            column = pl.multiple_of(tap * B + block * LANES, LANES)
            weights.append(staged[tile, :, pl.ds(column, LANES)])
            step = H - info[6 + tile] - tap
            column = pl.multiple_of((step // STEPS_PER_VREG) * LANES, LANES)
            windows.append(shifted[step % STEPS_PER_VREG, :, pl.ds(column, COLS)])
        left, right = jnp.concatenate(weights, 1), jnp.concatenate(windows, 0)
        total = jnp.dot(left, right, preferred_element_type=jnp.float32)
        if not first:
            total = total + before[tile]
        if not last:
            after[tile] = total
            continue
        total = total * info[8 + tile].astype(jnp.float32)
        core = info[2]
        for z in range(NZ):
            for h in range(NH):
                row = ((z * NH + h) * NC) * GROUP
                one, two = total[row : row + GROUP], total[row + GROUP : row + 2 * GROUP]
                keep[z, h, tile] = jnp.where(core == 0, one, two)
                send[z, h, tile] = jnp.where(core == 0, two, one)


def multiply(turn, info, kernel, low, high, before, last):
    first = before is None
    small = pl.BlockSpec(memory_space=pltpu.SMEM)
    near = pl.BlockSpec(memory_space=pltpu.VMEM)
    in_specs = [small, near, near, pl.BlockSpec(memory_space=pl.ANY) if first else near]
    operands = [info, low, high, kernel]
    scratch = [pltpu.VMEM((STEPS_PER_VREG, LANES, WIDE + COLS), jnp.bfloat16)]
    sums = jax.ShapeDtypeStruct((2, B, COLS), jnp.float32)
    if first:
        scratch.append(pltpu.SemaphoreType.DMA((2,)))
        out_specs, out_shape = [near, near], [sums, jax.ShapeDtypeStruct((2, B, TAPS * B), jnp.bfloat16)]
    else:
        in_specs.append(near)
        operands.append(before)
        out_specs, out_shape = near, sums
    if last:
        out_specs, out_shape = [near] * 2, [jax.ShapeDtypeStruct((NZ, NH, 2, GROUP, COLS), jnp.float32)] * 2
    return pl.pallas_call(
        lambda *refs: multiply_body(turn, first, last, *refs),
        in_specs=in_specs,
        out_specs=out_specs,
        out_shape=out_shape,
        scratch_shapes=scratch,
        input_output_aliases={} if first or last else {4: 0},
        compiler_params=pltpu.CompilerParams(vmem_limit_bytes=(40 if first else 32) << 20),
        cost_estimate=pl.CostEstimate(flops=4 * B * COLS * TAPS * LANES, transcendentals=0, bytes_accessed=4 << 20),
        name="multiply",
    )(*operands)


def power_of_two(exponent):
    size = jnp.abs(exponent)
    result = jnp.ones(exponent.shape, jnp.float32)
    for bit in range(7):
        up, down = float(2.0 ** (1 << bit)), float(2.0 ** -(1 << bit))
        factor = jnp.where(exponent < 0, down, up)
        result = jnp.where((size >> bit) & 1 == 1, result * factor, result)
    return result


def encode_body(info, keep, get, own, *messages):
    z, sign = info[3], info[4]
    own[...] = keep[z] + get[z]
    for offset, message in zip(OFFSETS, messages):
        there = (z + sign * offset + NZ) % NZ
        scales = []
        for group in range(NH * 2):
            h, t = divmod(group, 2)
            value = keep[there, h, t] + get[there, h, t]
            peak = jnp.max(jnp.abs(value), axis=(0, 1), keepdims=True)
            peak = jnp.broadcast_to(peak, (1, LANES))
            exponent = jnp.ceil(jnp.log2(jnp.maximum(peak, 1e-30))).astype(jnp.int32) - 15
            scales.append(exponent)
            inverse = jnp.broadcast_to(power_of_two(-exponent), (GROUP, LANES))
            for j in range(COLS // LANES):
                scaled = jnp.clip(jnp.round(value[:, j * LANES : (j + 1) * LANES] * inverse), -32767.0, 32767.0)
                row = (group * (COLS // LANES) + j) * GROUP
                message[row : row + GROUP] = scaled.astype(jnp.int32).astype(jnp.int16)
        rows = lax.broadcasted_iota(jnp.int32, (GROUP, LANES), 0) // 4
        packed = jnp.zeros((GROUP, LANES), jnp.int32)
        for group, exponent in enumerate(scales):
            packed = jnp.where(rows == group, jnp.broadcast_to(exponent, (GROUP, LANES)), packed)
        message[MESSAGE:] = packed.astype(jnp.int16)


def encode(info, keep, get):
    return pl.pallas_call(
        encode_body,
        in_specs=[pl.BlockSpec(memory_space=pltpu.SMEM)] + [pl.BlockSpec(memory_space=pltpu.VMEM)] * 2,
        out_shape=[jax.ShapeDtypeStruct((NH, 2, GROUP, COLS), jnp.float32)]
        + [jax.ShapeDtypeStruct((MESSAGE + GROUP, LANES), jnp.int16)] * len(OFFSETS),
        compiler_params=pltpu.CompilerParams(vmem_limit_bytes=24 << 20),
        name="encode",
    )(info, keep, get)


def decode_body(info, own, *refs):
    messages, mine, other = refs[: len(OFFSETS)], refs[-2], refs[-1]
    units = []
    for message in messages:
        packed = message[MESSAGE:].astype(jnp.int32)
        units.append([power_of_two(packed[4 * group : 4 * group + 1]) for group in range(NH * 2)])
    for t in range(2):
        for j in range(COLS // LANES):
            sums = []
            for h in range(NH):
                group = h * 2 + t
                row = (group * (COLS // LANES) + j) * GROUP
                total = own[h, t, :, j * LANES : (j + 1) * LANES]
                for message, unit in zip(messages, units):
                    part = message[row : row + GROUP].astype(jnp.int32).astype(jnp.float32)
                    total = total + part * jnp.broadcast_to(unit[group], (GROUP, LANES))
                sums.append(total)
            here = info[5] == 0
            mine[t, :, j * LANES : (j + 1) * LANES] = jnp.where(here, sums[0], sums[1])
            other[t, :, j * LANES : (j + 1) * LANES] = jnp.where(here, sums[1], sums[0])


def decode(info, own, messages):
    return pl.pallas_call(
        decode_body,
        in_specs=[pl.BlockSpec(memory_space=pltpu.SMEM)] + [pl.BlockSpec(memory_space=pltpu.VMEM)] * (1 + len(OFFSETS)),
        out_shape=[jax.ShapeDtypeStruct((2, GROUP, COLS), jnp.float32)] * 2,
        compiler_params=pltpu.CompilerParams(vmem_limit_bytes=24 << 20),
        name="decode",
    )(info, own, *messages)


def body(history, kernel, delays, tile_mask):
    y, xl, z, xh, c = (lax.axis_index(name) for name in AXES)
    delays, live = delays.reshape(2), tile_mask.reshape(2)
    here = history
    beside = shift(here, dx=1)
    up = shift(here, dy=1)
    down = shift(here, dy=-1)
    two = shift(here, dy=2)
    up_far = shift(beside, dy=1)
    down_far = shift(beside, dy=-1)
    two_far = shift(two, dx=1)

    info = jnp.stack([y, xl * 64, c, z, 1 - 2 * c, xh]).astype(jnp.int32)
    info = jnp.concatenate([info, delays, live])
    total, staged = multiply(0, info, kernel, here, beside, None, False)
    total = multiply(3, info, staged, up, up_far, total, False)
    total = multiply(1, info, staged, down, down_far, total, False)
    keep, send = multiply(2, info, staged, two, two_far, total, True)
    get = shift(send, dc=1)
    own, *messages = encode(info, keep, get)
    received = [shift(message, dz=offset) for offset, message in zip(OFFSETS, messages)]
    mine, other = decode(info, own, received)
    return mine + shift(other, dh=1)


def solution(mesh):
    fine = Mesh(mesh.devices.reshape(SHAPE), AXES)
    tgt, src = ("y", "xl"), ("z", "xh", "c")
    placed = (
        P(src + tgt, None),
        P(tgt, src, None, None),
        P(tgt, src),
        P(tgt, src),
    )
    return jax.shard_map(body, mesh=fine, in_specs=placed, out_specs=P(tgt, src, None), check_vma=False)
```

```python
import functools

import jax
import jax.numpy as jnp
import numpy as np
from jax import lax
from jax.experimental import pallas as pl
from jax.experimental.pallas import tpu as pltpu
from jax.sharding import Mesh, PartitionSpec as P

B = 512
TAPS = 8
H = 128
E = 16
S = 64
LANES = 128
COLS = S * E
WIDE = H * E
STEPS_PER_VREG = LANES // E

NY, NX, NZ, NH, NC = 4, 2, 8, 2, 2
AXES = ("y", "xl", "z", "xh", "c")
SHAPE = (NY, NX, NZ, NH, NC)
GROUP = 16
UNITS = 8
FIRST_LIMIT = 40
COLUMN_BLOCKS = COLS // LANES
UNIT_ROWS = GROUP * COLUMN_BLOCKS
SHIFTED = (STEPS_PER_VREG, LANES, WIDE + COLS)


def route(move):
    index = np.arange(np.prod(SHAPE)).reshape(SHAPE)
    pairs = []
    for here in np.ndindex(*SHAPE):
        there = tuple(p % n for p, n in zip(move(*here), SHAPE))
        pairs.append((int(index[here]), int(index[there])))
    return pairs


def shift(x, dy=0, dx=0, dz=0, dh=0, dc=0):
    def move(y, xl, z, xh, c):
        return (y + dy, xl + dx, z + (dz if c == 0 else -dz), xh + dh, c + dc)

    return lax.ppermute(x, AXES, route(move))


def build_tail(shifted):
    shifted[:, :, WIDE:] = jnp.zeros((STEPS_PER_VREG, LANES, COLS), jnp.bfloat16)


def build_rows(ref, place, shifted):
    value = ref[...]
    at = pl.multiple_of(place, 64)
    for j in range(STEPS_PER_VREG):
        moved = value if j == 0 else jnp.concatenate([value[:, j * E :], jnp.zeros((64, j * E), jnp.bfloat16)], 1)
        shifted[j, pl.ds(at, 64), :WIDE] = moved


def build_shifted(info, low, high, shifted):
    build_tail(shifted)
    build_rows(low, info[1], shifted)
    build_rows(high, 64 - info[1], shifted)


def product(info, tile, turns, staged, all_shifted):
    weights, windows = [], []
    for turn, shifted in zip(turns, all_shifted):
        block = lax.rem(info[0] + turn, NY)
        for tap in range(TAPS):
            column = pl.multiple_of(tap * B + block * LANES, LANES)
            weights.append(staged[tile, :, pl.ds(column, LANES)])
            step = H - info[6 + tile] - tap
            column = pl.multiple_of((step // STEPS_PER_VREG) * LANES, LANES)
            windows.append(shifted[step % STEPS_PER_VREG, :, pl.ds(column, COLS)])
    left, right = jnp.concatenate(weights, 1), jnp.concatenate(windows, 0)
    return jnp.dot(left, right, preferred_element_type=jnp.float32)


def split(info, tile, total, keep, send, sums):
    sums[...] = total * info[8 + tile].astype(jnp.float32)
    core, z, sign, xh = info[2], info[3], info[4], info[5]
    for target, core, sign in ((keep, core, sign), (send, 1 - core, -sign)):
        for unit in range(UNITS):
            offset = unit // 2 + 1 if unit < 6 else (4, 0)[unit - 6]
            there = lax.rem(z + sign * offset + NZ, NZ)
            owner = unit % 2 if unit < 6 else core
            for half, side in enumerate((xh, 1 - xh)):
                row = pl.multiple_of(((there * NH + side) * NC + owner) * GROUP, GROUP)
                target[half, unit] = sums[pl.ds(row, GROUP), :]


def first_body(info, low, high, kernel, sum0, sum1, staged, shifted, arrived):
    copies = [pltpu.make_async_copy(kernel.at[tile, 0], staged.at[tile], arrived.at[tile]) for tile in range(2)]
    for copy in copies:
        copy.start()
    build_shifted(info, low, high, shifted)
    for tile, after in enumerate((sum0, sum1)):
        copies[tile].wait()
        after[...] = product(info, tile, (0,), staged, (shifted,))


def middle_body(turn, info, low, high, staged, before, after, shifted):
    build_shifted(info, low, high, shifted)
    after[...] = before[...] + product(info, 0, (turn,), staged, (shifted,))


def last_body(turns, info, low0, high0, low1, high1, staged, before, keep, send, shifted0, shifted1, sums):
    build_shifted(info, low0, high0, shifted0)
    build_shifted(info, low1, high1, shifted1)
    total = before[...] + product(info, 0, turns, staged, (shifted0, shifted1))
    split(info, 0, total, keep, send, sums)


def rest_body(turns, info, staged, before, *refs):
    keep, send, sums = refs[-3:]
    split(info, 1, before[...] + product(info, 1, turns, staged, refs[: len(turns)]), keep, send, sums)


NEAR = pl.BlockSpec(memory_space=pltpu.VMEM)
SMALL = pl.BlockSpec(memory_space=pltpu.SMEM)
TOTAL = jax.ShapeDtypeStruct((B, COLS), jnp.float32)
PARTS = jax.ShapeDtypeStruct((NH, UNITS, GROUP, COLS), jnp.float32)
COPIES = jax.ShapeDtypeStruct(SHIFTED, jnp.bfloat16)


def call(run, outs, operands, scratch=(), specs=None, limit=16, blocks=0, aliases=None):
    return pl.pallas_call(
        run,
        in_specs=specs or [SMALL] + [NEAR] * (len(operands) - 1),
        out_specs=[NEAR] * len(outs),
        out_shape=outs,
        scratch_shapes=scratch,
        input_output_aliases=aliases or {},
        compiler_params=pltpu.CompilerParams(vmem_limit_bytes=limit << 20),
        cost_estimate=pl.CostEstimate(
            flops=2 * B * COLS * TAPS * LANES * blocks, transcendentals=0, bytes_accessed=(4 << 20) if blocks else (1 << 20)
        ),
    )(*operands)


def power_of_two(exponent):
    size = jnp.abs(exponent)
    result = jnp.ones(exponent.shape, jnp.float32)
    for bit in range(7):
        up, down = float(2.0 ** (1 << bit)), float(2.0 ** -(1 << bit))
        factor = jnp.where(exponent < 0, down, up)
        result = jnp.where((size >> bit) & 1 == 1, result * factor, result)
    return result


def put(message, groups):
    exponents = []
    for index, value in enumerate(groups):
        peak = jnp.max(jnp.abs(value), axis=(0, 1), keepdims=True)
        peak = jnp.broadcast_to(peak, (1, LANES))
        exponent = jnp.ceil(jnp.log2(jnp.maximum(peak, 1e-30))).astype(jnp.int32) - 15
        exponents.append(exponent)
        inverse = jnp.broadcast_to(power_of_two(-exponent), (GROUP, LANES))
        for j in range(COLUMN_BLOCKS):
            scaled = jnp.clip(jnp.round(value[:, j * LANES : (j + 1) * LANES] * inverse), -32767.0, 32767.0)
            row = index * UNIT_ROWS + j * GROUP
            message[row : row + GROUP] = scaled.astype(jnp.int32).astype(jnp.int16)
    rows = lax.broadcasted_iota(jnp.int32, (GROUP, LANES), 0) // 2
    packed = jnp.zeros((GROUP, LANES), jnp.int32)
    for index, exponent in enumerate(exponents):
        packed = jnp.where(rows == index, jnp.broadcast_to(exponent, (GROUP, LANES)), packed)
    message[len(groups) * UNIT_ROWS :] = packed.astype(jnp.int16)


def units_of(message, count):
    packed = message[count * UNIT_ROWS :].astype(jnp.int32)
    return [jnp.broadcast_to(power_of_two(packed[2 * index : 2 * index + 1]), (GROUP, LANES)) for index in range(count)]


def part(message, unit, index, j):
    row = index * UNIT_ROWS + j * GROUP
    return message[row : row + GROUP].astype(jnp.int32).astype(jnp.float32) * unit[index]


def sent(count):
    return jax.ShapeDtypeStruct((count * UNIT_ROWS + GROUP, LANES), jnp.int16)


def across_body(info, keep, get, own, message):
    own[...] = keep[0] + get[0]
    put(message, [keep[1, unit] + get[1, unit] for unit in range(UNITS)])


def both_body(info, keep, get, one, two, three, four, base):
    def value(half, unit):
        return keep[half, unit] + get[half, unit]

    for k, message in enumerate((one, two, three)):
        put(message, [value(half, 2 * k + owner) for owner in range(2) for half in range(NH)])
    put(four, [value(half, 6) for half in range(NH)])
    for half in range(NH):
        base[half] = value(half, 7)


def along_body(info, own, come, one, two, three, four, base):
    unit = units_of(come, UNITS)

    def value(u):
        parts = [own[u, :, j * LANES : (j + 1) * LANES] + part(come, unit, u, j) for j in range(COLUMN_BLOCKS)]
        return jnp.concatenate(parts, 1)

    for k, message in enumerate((one, two, three)):
        put(message, [value(2 * k + owner) for owner in range(2)])
    put(four, [value(6)])
    base[...] = value(7)


def gather_body(info, base, one, two, three, four, stay, cross):
    units = [units_of(message, 4) for message in (one, two, three)]
    last = units_of(four, 2)
    for half, target in enumerate((stay, cross)):
        for j in range(COLUMN_BLOCKS):
            lanes = slice(j * LANES, (j + 1) * LANES)
            here = base[half, :, lanes] + part(four, last, half, j)
            for owner in range(2):
                parts = [part(m, u, owner * 2 + half, j) for m, u in zip((one, two, three), units)]
                extra = jnp.where(info[2] == owner, here, jnp.zeros_like(here))
                target[owner, :, lanes] = parts[0] + parts[1] + parts[2] + extra


def finish_body(info, base, stay, got, one, two, three, four, mine, other):
    core = info[2]
    units = [units_of(message, 2) for message in (one, two, three)]
    last = units_of(four, 1)
    for j in range(COLUMN_BLOCKS):
        lanes = slice(j * LANES, (j + 1) * LANES)
        sums, done = [], []
        for owner in range(2):
            parts = [part(m, u, owner, j) for m, u in zip((one, two, three), units)]
            sums.append(parts[0] + parts[1] + parts[2])
            done.append(stay[owner, :, lanes] + got[owner, :, lanes])
        here = base[:, lanes] + part(four, last, 0, j)
        mine[0, :, lanes] = jnp.where(core == 0, sums[0], sums[1]) + here
        other[0, :, lanes] = jnp.where(core == 0, sums[1], sums[0])
        mine[1, :, lanes] = jnp.where(core == 0, done[0], done[1])
        other[1, :, lanes] = jnp.where(core == 0, done[1], done[0])


def compute(history, kernel, delays, tile_mask):
    y, xl, z, xh, c = (lax.axis_index(name) for name in AXES)
    delays, live = delays.reshape(2), tile_mask.reshape(2)
    here = history
    beside = shift(here, dx=1)
    up = shift(here, dy=1)
    down = shift(here, dy=-1)
    two = shift(here, dy=2)
    up_far = shift(beside, dy=1)
    down_far = shift(beside, dy=-1)
    two_far = shift(two, dx=1)

    info = jnp.stack([y, xl * 64, c, z, 1 - 2 * c, xh]).astype(jnp.int32)
    info = jnp.concatenate([info, delays, live])
    sum0, sum1, staged = call(
        first_body,
        [TOTAL, TOTAL, jax.ShapeDtypeStruct((2, B, TAPS * B), jnp.bfloat16)],
        [info, here, beside, kernel],
        [pltpu.VMEM(SHIFTED, jnp.bfloat16), pltpu.SemaphoreType.DMA((2,))],
        [SMALL, NEAR, NEAR, pl.BlockSpec(memory_space=pl.ANY)],
        FIRST_LIMIT,
        2,
    )
    run = functools.partial(middle_body, 2)
    operands = [info, two, two_far, staged, sum0]
    sum0, two_copies = call(run, [TOTAL, COPIES], operands, blocks=1, aliases={4: 0})
    sums = [pltpu.VMEM((B, COLS), jnp.float32)]
    run = functools.partial(last_body, (3, 1))
    operands = [info, up, up_far, down, down_far, staged, sum0]
    keep0, send0, up_copies, down_copies = call(run, [PARTS, PARTS, COPIES, COPIES], operands, sums, blocks=2)
    get0 = shift(send0, dc=1)
    run = functools.partial(rest_body, (2, 3, 1))
    operands = [info, staged, sum1, two_copies, up_copies, down_copies]
    keep1, send1 = call(run, [PARTS, PARTS], operands, sums, blocks=3)
    get1 = shift(send1, dc=1)
    rows = jax.ShapeDtypeStruct((UNITS, GROUP, COLS), jnp.float32)
    own0, go0 = call(across_body, [rows, sent(UNITS)], [info, keep0, get0])
    come0 = shift(go0, dh=1)
    pair = jax.ShapeDtypeStruct((2, GROUP, COLS), jnp.float32)
    single = jax.ShapeDtypeStruct((GROUP, COLS), jnp.float32)
    *messages, base1 = call(both_body, [sent(4)] * 3 + [sent(2), pair], [info, keep1, get1])
    came1 = [shift(message, dz=offset) for offset, message in zip((1, 2, 3, 4), messages)]
    *messages, base0 = call(along_body, [sent(2)] * 3 + [sent(1), single], [info, own0, come0])
    came0 = [shift(message, dz=offset) for offset, message in zip((1, 2, 3, 4), messages)]
    stay, cross = call(gather_body, [pair, pair], [info, base1, *came1])
    got = shift(cross, dh=1)
    mine, other = call(finish_body, [pair, pair], [info, base0, stay, got, *came0])
    return mine + shift(other, dc=1)


def solution(mesh):
    fine = Mesh(mesh.devices.reshape(SHAPE), AXES)
    tgt, src = ("y", "xl"), ("z", "xh", "c")
    placed = (
        P(src + tgt, None),
        P(tgt, src, None, None),
        P(tgt, src),
        P(tgt, src),
    )
    return jax.shard_map(compute, mesh=fine, in_specs=placed, out_specs=P(tgt, src, None), check_vma=False)
```

```python
import functools

import jax
import jax.numpy as jnp
import numpy as np
from jax import lax
from jax.experimental import pallas as pl
from jax.experimental.pallas import tpu as pltpu
from jax.sharding import Mesh, PartitionSpec as P

B = 512
TAPS = 8
H = 128
E = 16
S = 64
LANES = 128
COLS = S * E
WIDE = H * E
STEPS_PER_VREG = LANES // E

NY, NX, NZ, NH, NC = 4, 2, 8, 2, 2
AXES = ("y", "xl", "z", "xh", "c")
SHAPE = (NY, NX, NZ, NH, NC)
GROUP = 16
UNITS = 8
FIRST_LIMIT = 40
COLUMN_BLOCKS = COLS // LANES
UNIT_ROWS = GROUP * COLUMN_BLOCKS
SHIFTED = (STEPS_PER_VREG, LANES, WIDE + COLS)


def route(move):
    index = np.arange(np.prod(SHAPE)).reshape(SHAPE)
    pairs = []
    for here in np.ndindex(*SHAPE):
        there = tuple(p % n for p, n in zip(move(*here), SHAPE))
        pairs.append((int(index[here]), int(index[there])))
    return pairs


def shift(x, dy=0, dx=0, dz=0, dh=0, dc=0):
    def move(y, xl, z, xh, c):
        return (y + dy, xl + dx, z + (dz if c == 0 else -dz), xh + dh, c + dc)

    return lax.ppermute(x, AXES, route(move))


def build_tail(shifted):
    shifted[:, :, WIDE:] = jnp.zeros((STEPS_PER_VREG, LANES, COLS), jnp.bfloat16)


def build_rows(ref, place, shifted):
    value = ref[...]
    at = pl.multiple_of(place, 64)
    for j in range(STEPS_PER_VREG):
        moved = value if j == 0 else jnp.concatenate([value[:, j * E :], jnp.zeros((64, j * E), jnp.bfloat16)], 1)
        shifted[j, pl.ds(at, 64), :WIDE] = moved


def build_shifted(info, low, high, shifted):
    build_tail(shifted)
    build_rows(low, info[1], shifted)
    build_rows(high, 64 - info[1], shifted)


def product(info, tile, turns, staged, all_shifted):
    weights, windows = [], []
    for turn, shifted in zip(turns, all_shifted):
        block = lax.rem(info[0] + turn, NY)
        for tap in range(TAPS):
            column = pl.multiple_of(tap * B + block * LANES, LANES)
            weights.append(staged[tile, :, pl.ds(column, LANES)])
            step = H - info[6 + tile] - tap
            column = pl.multiple_of((step // STEPS_PER_VREG) * LANES, LANES)
            windows.append(shifted[step % STEPS_PER_VREG, :, pl.ds(column, COLS)])
    left, right = jnp.concatenate(weights, 1), jnp.concatenate(windows, 0)
    return jnp.dot(left, right, preferred_element_type=jnp.float32)


def split(info, tile, total, keep, send, sums):
    sums[...] = total * info[8 + tile].astype(jnp.float32)
    core, z, sign, xh = info[2], info[3], info[4], info[5]
    for target, core, sign in ((keep, core, sign), (send, 1 - core, -sign)):
        for unit in range(UNITS):
            offset = unit // 2 + 1 if unit < 6 else (4, 0)[unit - 6]
            there = lax.rem(z + sign * offset + NZ, NZ)
            owner = unit % 2 if unit < 6 else core
            for half, side in enumerate((xh, 1 - xh)):
                row = pl.multiple_of(((there * NH + side) * NC + owner) * GROUP, GROUP)
                target[half, unit] = sums[pl.ds(row, GROUP), :]


def first_body(info, low, high, kernel, sum0, sum1, staged, shifted, arrived):
    copies = [pltpu.make_async_copy(kernel.at[tile, 0], staged.at[tile], arrived.at[tile]) for tile in range(2)]
    for copy in copies:
        copy.start()
    build_shifted(info, low, high, shifted)
    for tile, after in enumerate((sum0, sum1)):
        copies[tile].wait()
        after[...] = product(info, tile, (0,), staged, (shifted,))


def last_body(turns, info, *refs):
    count = len(turns)
    sources, (staged, before, keep, send) = refs[: 2 * count], refs[2 * count : 2 * count + 4]
    copies, sums = refs[2 * count + 4 : -1], refs[-1]
    for index, shifted in enumerate(copies):
        build_shifted(info, sources[2 * index], sources[2 * index + 1], shifted)
    split(info, 0, before[...] + product(info, 0, turns, staged, copies), keep, send, sums)


def rest_body(turns, info, staged, before, *refs):
    keep, send, sums = refs[-3:]
    split(info, 1, before[...] + product(info, 1, turns, staged, refs[: len(turns)]), keep, send, sums)


NEAR = pl.BlockSpec(memory_space=pltpu.VMEM)
SMALL = pl.BlockSpec(memory_space=pltpu.SMEM)
TOTAL = jax.ShapeDtypeStruct((B, COLS), jnp.float32)
PARTS = jax.ShapeDtypeStruct((NH, UNITS, GROUP, COLS), jnp.float32)
COPIES = jax.ShapeDtypeStruct(SHIFTED, jnp.bfloat16)


def call(run, outs, operands, scratch=(), specs=None, limit=16, blocks=0, aliases=None):
    return pl.pallas_call(
        run,
        in_specs=specs or [SMALL] + [NEAR] * (len(operands) - 1),
        out_specs=[NEAR] * len(outs),
        out_shape=outs,
        scratch_shapes=scratch,
        input_output_aliases=aliases or {},
        compiler_params=pltpu.CompilerParams(vmem_limit_bytes=limit << 20),
        cost_estimate=pl.CostEstimate(
            flops=2 * B * COLS * TAPS * LANES * blocks, transcendentals=0, bytes_accessed=(4 << 20) if blocks else (1 << 20)
        ),
    )(*operands)


def power_of_two(exponent):
    size = jnp.abs(exponent)
    result = jnp.ones(exponent.shape, jnp.float32)
    for bit in range(7):
        up, down = float(2.0 ** (1 << bit)), float(2.0 ** -(1 << bit))
        factor = jnp.where(exponent < 0, down, up)
        result = jnp.where((size >> bit) & 1 == 1, result * factor, result)
    return result


def put(message, groups):
    exponents = []
    for index, value in enumerate(groups):
        peak = jnp.max(jnp.abs(value), axis=(0, 1), keepdims=True)
        peak = jnp.broadcast_to(peak, (1, LANES))
        exponent = jnp.ceil(jnp.log2(jnp.maximum(peak, 1e-30))).astype(jnp.int32) - 15
        exponents.append(exponent)
        inverse = jnp.broadcast_to(power_of_two(-exponent), (GROUP, LANES))
        for j in range(COLUMN_BLOCKS):
            scaled = jnp.clip(jnp.round(value[:, j * LANES : (j + 1) * LANES] * inverse), -32767.0, 32767.0)
            row = index * UNIT_ROWS + j * GROUP
            message[row : row + GROUP] = scaled.astype(jnp.int32).astype(jnp.int16)
    rows = lax.broadcasted_iota(jnp.int32, (GROUP, LANES), 0) // 2
    packed = jnp.zeros((GROUP, LANES), jnp.int32)
    for index, exponent in enumerate(exponents):
        packed = jnp.where(rows == index, jnp.broadcast_to(exponent, (GROUP, LANES)), packed)
    message[len(groups) * UNIT_ROWS :] = packed.astype(jnp.int16)


def units_of(message, count):
    packed = message[count * UNIT_ROWS :].astype(jnp.int32)
    return [jnp.broadcast_to(power_of_two(packed[2 * index : 2 * index + 1]), (GROUP, LANES)) for index in range(count)]


def part(message, unit, index, j):
    row = index * UNIT_ROWS + j * GROUP
    return message[row : row + GROUP].astype(jnp.int32).astype(jnp.float32) * unit[index]


def sent(count):
    return jax.ShapeDtypeStruct((count * UNIT_ROWS + GROUP, LANES), jnp.int16)


def across_body(info, keep, get, own, message):
    own[...] = keep[0] + get[0]
    put(message, [keep[1, unit] + get[1, unit] for unit in range(UNITS)])


def both_body(info, keep, get, one, two, three, four, base):
    def value(half, unit):
        return keep[half, unit] + get[half, unit]

    for k, message in enumerate((one, two, three)):
        put(message, [value(half, 2 * k + owner) for owner in range(2) for half in range(NH)])
    put(four, [value(half, 6) for half in range(NH)])
    for half in range(NH):
        base[half] = value(half, 7)


def along_body(info, own, come, one, two, three, four, base):
    unit = units_of(come, UNITS)

    def value(u):
        parts = [own[u, :, j * LANES : (j + 1) * LANES] + part(come, unit, u, j) for j in range(COLUMN_BLOCKS)]
        return jnp.concatenate(parts, 1)

    for k, message in enumerate((one, two, three)):
        put(message, [value(2 * k + owner) for owner in range(2)])
    put(four, [value(6)])
    base[...] = value(7)


def gather_body(info, base, one, two, three, four, stay, cross):
    units = [units_of(message, 4) for message in (one, two, three)]
    last = units_of(four, 2)
    for half, target in enumerate((stay, cross)):
        for j in range(COLUMN_BLOCKS):
            lanes = slice(j * LANES, (j + 1) * LANES)
            here = base[half, :, lanes] + part(four, last, half, j)
            for owner in range(2):
                parts = [part(m, u, owner * 2 + half, j) for m, u in zip((one, two, three), units)]
                extra = jnp.where(info[2] == owner, here, jnp.zeros_like(here))
                target[owner, :, lanes] = parts[0] + parts[1] + parts[2] + extra


def finish_body(info, base, stay, got, one, two, three, four, mine, other):
    core = info[2]
    units = [units_of(message, 2) for message in (one, two, three)]
    last = units_of(four, 1)
    for j in range(COLUMN_BLOCKS):
        lanes = slice(j * LANES, (j + 1) * LANES)
        sums, done = [], []
        for owner in range(2):
            parts = [part(m, u, owner, j) for m, u in zip((one, two, three), units)]
            sums.append(parts[0] + parts[1] + parts[2])
            done.append(stay[owner, :, lanes] + got[owner, :, lanes])
        here = base[:, lanes] + part(four, last, 0, j)
        mine[0, :, lanes] = jnp.where(core == 0, sums[0], sums[1]) + here
        other[0, :, lanes] = jnp.where(core == 0, sums[1], sums[0])
        mine[1, :, lanes] = jnp.where(core == 0, done[0], done[1])
        other[1, :, lanes] = jnp.where(core == 0, done[1], done[0])


def compute(history, kernel, delays, tile_mask):
    y, xl, z, xh, c = (lax.axis_index(name) for name in AXES)
    delays, live = delays.reshape(2), tile_mask.reshape(2)
    here = history
    beside = shift(here, dx=1)
    up = shift(here, dy=1)
    down = shift(here, dy=-1)
    two = shift(here, dy=2)
    up_far = shift(beside, dy=1)
    down_far = shift(beside, dy=-1)
    two_far = shift(two, dx=1)

    info = jnp.stack([y, xl * 64, c, z, 1 - 2 * c, xh]).astype(jnp.int32)
    info = jnp.concatenate([info, delays, live])
    sum0, sum1, staged = call(
        first_body,
        [TOTAL, TOTAL, jax.ShapeDtypeStruct((2, B, TAPS * B), jnp.bfloat16)],
        [info, here, beside, kernel],
        [pltpu.VMEM(SHIFTED, jnp.bfloat16), pltpu.SemaphoreType.DMA((2,))],
        [SMALL, NEAR, NEAR, pl.BlockSpec(memory_space=pl.ANY)],
        FIRST_LIMIT,
        2,
    )
    sums = [pltpu.VMEM((B, COLS), jnp.float32)]
    run = functools.partial(last_body, (2, 3, 1))
    operands = [info, two, two_far, up, up_far, down, down_far, staged, sum0]
    outs = [PARTS, PARTS, COPIES, COPIES, COPIES]
    keep0, send0, two_copies, up_copies, down_copies = call(run, outs, operands, sums, blocks=3)
    get0 = shift(send0, dc=1)
    run = functools.partial(rest_body, (2, 3, 1))
    operands = [info, staged, sum1, two_copies, up_copies, down_copies]
    keep1, send1 = call(run, [PARTS, PARTS], operands, sums, blocks=3)
    get1 = shift(send1, dc=1)
    rows = jax.ShapeDtypeStruct((UNITS, GROUP, COLS), jnp.float32)
    own0, go0 = call(across_body, [rows, sent(UNITS)], [info, keep0, get0])
    come0 = shift(go0, dh=1)
    pair = jax.ShapeDtypeStruct((2, GROUP, COLS), jnp.float32)
    single = jax.ShapeDtypeStruct((GROUP, COLS), jnp.float32)
    *messages, base1 = call(both_body, [sent(4)] * 3 + [sent(2), pair], [info, keep1, get1])
    came1 = [shift(message, dz=offset) for offset, message in zip((1, 2, 3, 4), messages)]
    *messages, base0 = call(along_body, [sent(2)] * 3 + [sent(1), single], [info, own0, come0])
    came0 = [shift(message, dz=offset) for offset, message in zip((1, 2, 3, 4), messages)]
    stay, cross = call(gather_body, [pair, pair], [info, base1, *came1])
    got = shift(cross, dh=1)
    mine, other = call(finish_body, [pair, pair], [info, base0, stay, got, *came0])
    return mine + shift(other, dc=1)


def solution(mesh):
    fine = Mesh(mesh.devices.reshape(SHAPE), AXES)
    tgt, src = ("y", "xl"), ("z", "xh", "c")
    placed = (
        P(src + tgt, None),
        P(tgt, src, None, None),
        P(tgt, src),
        P(tgt, src),
    )
    return jax.shard_map(compute, mesh=fine, in_specs=placed, out_specs=P(tgt, src, None), check_vma=False)
```
